128 devices in a mesh: tm: 64 (over x, z, y), head: 2 (over core).
Axes of the slice: x: 4, y: 4, z: 4, core: 2. Of those that a mesh axis runs over, the one named last changes fastest.
Arguments:
- series: bfloat16 [16, 65536, 512], P(None, 'tm'), may hold values from -6 to 6
- modes: int32 [128], replicated, may hold values from 1 to 32767, as said below
- query_weight: bfloat16 [512, 512], P(None, 'head'), may hold values from -0.25 to 0.25
- mix_weight: float32 [128, 8, 64, 128], P('tm', 'head'), may hold values from -0.5 to 0.5
- out_weight: bfloat16 [512, 512], P(None, 'head'), may hold values from -0.25 to 0.25
Outputs:
- output: bfloat16 [16, 65536, 512], P(None, 'tm', 'head')
The draws below stay inside these ranges and needn't reach their ends.
Inputs may be any that keep to these rules, and one draw needn't show every extreme that they name: `modes`: distinct mode numbers; both 1 and one less than half of 65536 are among them.
All inputs are finite; a program needn't handle non-finite values.
Results may differ from the reference program's by a relative error of at most 0.0075.
Values may be sent and summed in bfloat16 or wider, within the bound.
A program may use at most 128 MiB of HBM per device.

```python
import math
import jax
import jax.numpy as jnp
from jax import lax

D = 512
H = 8
M = 128
SEQS = 16
E = 64
LENGTH = 65536


def draw_modes(key, part):
    half_length = LENGTH // 2
    inner_modes = jax.random.permutation(key, half_length - 3).astype(jnp.int32) + 2
    chosen = jnp.concatenate([jnp.array([1, half_length - 1], jnp.int32), inner_modes[:M - 2]])
    shuffle = jax.random.permutation(jax.random.fold_in(key, 7), M)
    return chosen[shuffle]


def block_levels(rng, extent, pieces, least, high):
    def one(dim, blocks):
        steps = jax.random.uniform(jax.random.fold_in(jax.random.fold_in(rng, 6), dim), (blocks,), jnp.float32, least / len(pieces), high / len(pieces))
        return jnp.repeat(jnp.exp(steps), extent[dim] // blocks).reshape((-1,) + (1,) * (len(extent) - dim - 1))

    level = one(*pieces[0])
    for cut in pieces[1:]:
        level = level * one(*cut)
    return level


def scatter_about(stream_key, dims, spread, bound, pieces=(), kind=jnp.bfloat16):
    drawn = jax.random.normal(stream_key, dims, jnp.float32) * spread
    if len(pieces) > 0:
        drawn = block_levels(stream_key, dims, pieces, -0.22, 0.18) * drawn
    return jnp.clip(drawn, min=-bound, max=bound).astype(kind)


def setup_inputs(seed: int = 0) -> dict:
    streams_of = jax.random.split(jax.random.key(seed), 6)
    return {
        "series": scatter_about(streams_of[0], (SEQS, LENGTH, D), 1.0, 6.0, ((1, 64),)),
        "modes": draw_modes(jax.random.fold_in(streams_of[5], 71), 0),
        "query_weight": scatter_about(streams_of[2], (D, D), D ** -0.5, 0.25, ((1, 2),)),
        "mix_weight": scatter_about(streams_of[3], (M, H, E, 2 * E), (2 * E) ** -0.5, 0.5, ((0, 64), (1, 2)), jnp.float32),
        "out_weight": scatter_about(streams_of[4], (D, D), D ** -0.5, 0.25, ((1, 2),)),
    }


two_pi = 2.0 * math.pi

def wave_tables(mode_list, first_time, time_count, series_length):
    time_index = first_time + lax.iota(jnp.int32, time_count)
    phases = time_index[:, None] * mode_list[None, :] % series_length
    angles = phases.astype(jnp.float32) * (two_pi / series_length)
    return (jnp.cos(angles).astype(jnp.bfloat16), jnp.sin(angles).astype(jnp.bfloat16))

def reference(series, modes, query_weight, mix_weight, out_weight):
    series_count = series.shape[0]
    block_rows = min(LENGTH, 8192)
    block_total = LENGTH // block_rows
    forward_scale = 1.0 / math.sqrt(LENGTH)
    inverse_scale = 1.0 / math.sqrt(M)
    highest = lax.Precision.HIGHEST
    block_ids = jnp.arange(block_total, dtype=jnp.int32)

    def forward_block(running, block_index):
        first_time = (block_index * block_rows).astype(jnp.int32)
        block_series = lax.dynamic_slice_in_dim(series, first_time, block_rows, 1)
        queries = jnp.dot(block_series.reshape(-1, D), query_weight, preferred_element_type=jnp.float32)
        queries = queries.astype(jnp.bfloat16).reshape(series_count, block_rows, D).astype(jnp.float32)
        cosine, sine_part = wave_tables(modes, first_time, block_rows, LENGTH)
        real_part = jnp.einsum('tm,btf->mbf', cosine.astype(jnp.float32), queries, precision=highest)
        imag_part = jnp.einsum('tm,btf->mbf', sine_part.astype(jnp.float32), queries, precision=highest)
        return (running + jnp.stack([real_part, -imag_part], axis=1) * forward_scale, None)
    spectrum, _ = lax.scan(forward_block, jnp.zeros((M, 2, series_count, D), jnp.float32), block_ids)
    spec_parts = spectrum.reshape(M, 2, series_count, H, E)
    from_real = jnp.einsum('mbhi,mhio->mbho', spec_parts[:, 0], mix_weight, precision=highest)
    from_imag = jnp.einsum('mbhi,mhio->mbho', spec_parts[:, 1], mix_weight, precision=highest)
    mixed_real = from_real[..., :E] - from_imag[..., E:]
    mixed_imag = from_real[..., E:] + from_imag[..., :E]
    mixed_spectra = jnp.stack([mixed_real, mixed_imag], axis=1).reshape(M, 2, series_count, D)
    mixed_spectra = mixed_spectra.astype(jnp.bfloat16).astype(jnp.float32)

    def inverse_block(running, block_index):
        first_time = (block_index * block_rows).astype(jnp.int32)
        cosine, sine_part = wave_tables(modes, first_time, block_rows, LENGTH)
        summed = jnp.einsum('tm,mbf->btf', cosine.astype(jnp.float32), mixed_spectra[:, 0], precision=highest)
        summed = summed - jnp.einsum('tm,mbf->btf', sine_part.astype(jnp.float32), mixed_spectra[:, 1], precision=highest)
        restored = (summed * inverse_scale).astype(jnp.bfloat16)
        output = jnp.dot(restored.reshape(-1, D), out_weight, preferred_element_type=jnp.float32)
        return (running, output.astype(jnp.bfloat16).reshape(series_count, block_rows, D))
    _, stacked = lax.scan(inverse_block, jnp.zeros((), jnp.float32), block_ids)
    return jnp.moveaxis(stacked, 0, 1).reshape(series_count, LENGTH, D)
```

```python
import math

import jax
import jax.numpy as jnp
from jax import lax
from jax.sharding import PartitionSpec as P

two_pi = 2.0 * math.pi


def wave_table(mode_list, first_time, time_count, series_length):
    time_index = first_time + lax.iota(jnp.int32, time_count)
    phases = time_index[:, None] * mode_list[None, :] % series_length
    angles = phases.astype(jnp.float32) * (two_pi / series_length)
    waves = jnp.stack([jnp.cos(angles), -jnp.sin(angles)], axis=2)
    return waves.astype(jnp.bfloat16).reshape(time_count, -1)


def body(series, modes, query_weight, mix_weight, out_weight):
    series_count, shard_rows, model_width = series.shape
    group_width = query_weight.shape[1]
    mode_total = modes.shape[0]
    own_modes, heads_here, head_size, _ = mix_weight.shape
    head_groups = lax.axis_size("head")
    own_series = series_count // head_groups
    series_length = lax.axis_size("tm") * shard_rows
    first_time = lax.axis_index("tm") * shard_rows
    forward_scale = 1.0 / math.sqrt(series_length)
    inverse_scale = 1.0 / math.sqrt(mode_total)
    highest = lax.Precision.HIGHEST
    mine = lax.dynamic_slice_in_dim(series, lax.axis_index("head") * own_series, own_series, 0)
    table = wave_table(modes, first_time, shard_rows, series_length)
    partial = jnp.einsum("tk,btd->kbd", table, mine, preferred_element_type=jnp.float32)
    summed = lax.psum_scatter(partial * forward_scale, "tm", scatter_dimension=0, tiled=True)
    summed = lax.all_gather(summed, "head", axis=1, tiled=True)
    spectrum = jnp.einsum("kbd,df->kbf", summed, query_weight.astype(jnp.float32), precision=highest)
    parts = spectrum.reshape(own_modes, 2, series_count, heads_here, head_size)
    from_real = jnp.einsum("mbhi,mhio->mbho", parts[:, 0], mix_weight, precision=highest)
    from_imag = jnp.einsum("mbhi,mhio->mbho", parts[:, 1], mix_weight, precision=highest)
    mixed_real = from_real[..., :head_size] - from_imag[..., head_size:]
    mixed_imag = from_real[..., head_size:] + from_imag[..., :head_size]
    mixed = jnp.stack([mixed_real, mixed_imag], axis=1).astype(jnp.bfloat16)
    mixed = mixed.reshape(2 * own_modes, series_count, group_width)
    mixed = lax.all_gather(mixed, "head", axis=2, tiled=True)
    projected = jnp.einsum("kbf,fo->kbo", mixed, out_weight, preferred_element_type=jnp.float32)
    projected = (projected * inverse_scale).astype(jnp.bfloat16)
    everything = lax.all_gather(projected, "tm", axis=0, tiled=True)
    output = jnp.einsum("tk,kbo->bto", table, everything, preferred_element_type=jnp.float32)
    return output.astype(jnp.bfloat16)


def solution(mesh):
    in_specs = (
        P(None, "tm", None),
        P(),
        P(None, "head"),
        P("tm", "head", None, None),
        P(None, "head"),
    )
    out_specs = P(None, "tm", "head")
    return jax.shard_map(body, mesh=mesh, in_specs=in_specs, out_specs=out_specs, check_vma=False)
```

```python
import functools
import math

import jax
import jax.numpy as jnp
from jax import lax
from jax.experimental import pallas as pl
from jax.experimental.pallas import tpu as pltpu
from jax.sharding import PartitionSpec as P

F32 = jnp.float32
BF16 = jnp.bfloat16
MESH = pl.DeviceIdType.MESH
RING = 4
PARTS = 3
PERIOD = 65536


def iota(shape, dim):
    return lax.broadcasted_iota(jnp.int32, shape, dim)


def one_hot(shape, wanted):
    return (iota(shape, 1) == wanted).astype(F32).astype(BF16)


def dot(a, b):
    return jnp.dot(a, b, preferred_element_type=F32)


def dot_nt(a, b):
    return lax.dot_general(a, b, (((1,), (1,)), ((), ())), preferred_element_type=F32)


def cos_sin(phase):
    phase = phase & (PERIOD - 1)
    quarter = (phase + PERIOD // 8) >> 14
    r = (phase - (quarter << 14)).astype(F32) * (2.0 * math.pi / PERIOD)
    q = r * r
    s = r * (1.0 + q * (-1 / 6 + q * (1 / 120 + q * (-1 / 5040 + q * (1 / 362880)))))
    c = 1.0 + q * (-0.5 + q * (1 / 24 + q * (-1 / 720 + q * (1 / 40320))))
    odd = (quarter & 1) == 1
    cos_value = jnp.where(odd, s, c)
    sin_value = jnp.where(odd, c, s)
    cos_value = jnp.where(((quarter + 1) & 2) != 0, -cos_value, cos_value)
    sin_value = jnp.where((quarter & 2) != 0, -sin_value, sin_value)
    return cos_value, sin_value


def stride_of(axis):
    return 16 - 12 * axis + 9 * ((axis * (axis - 1)) // 2)


def split(x):
    high = x.astype(BF16)
    low = (x - high.astype(F32)).astype(BF16)
    return high, low


def order_row(k, part):
    first, second, third, r = k // 64, (k // 16) % 4, (k // 4) % 4, k % 4
    if part == 0:
        return k
    if part == 1:
        return third * 64 + first * 16 + second * 4 + r
    return second * 64 + third * 16 + first * 4 + r


def exchange_kernel(
    scale, series, modes, wq_in, mix_in, wo_in, tab_out, gat_out,
    x, table, wide, sent, ra, rb, acc, s2, r2, v3, s3, r3, xs, wq, mix, wo, mw, mx, a1, gb,
    x_sem, w_sem, o_sem, p_send, p_recv, send1, recv1, send2, recv2, send3, recv3,
    g1_send, g1_recv, g2_send, g2_recv, g3_send, g3_recv,
):
    tm = lax.axis_index("tm")
    h = lax.axis_index("head")
    count = x.shape[0]

    def coord(axis):
        return lax.rem(lax.div(tm, stride_of(axis)), RING)

    def along(axis, distance):
        c = coord(axis)
        return tm + (lax.rem(c + distance, RING) - c) * stride_of(axis)

    def remote(src, dst, ssem, rsem, target):
        return pltpu.make_async_remote_copy(
            src_ref=src, dst_ref=dst, send_sem=ssem, recv_sem=rsem,
            device_id=(target, h), device_id_type=MESH,
        )

    def to_partner(src, dst, k):
        return pltpu.make_async_remote_copy(
            src_ref=src, dst_ref=dst, send_sem=p_send.at[k], recv_sem=p_recv.at[k],
            device_id=(tm, 1 - h), device_id_type=MESH,
        )

    def load_x(s):
        return pltpu.make_async_copy(series.at[h * count + s], x.at[s], x_sem.at[s])

    loads = [
        pltpu.make_async_copy(wq_in, wq.at[0], w_sem.at[0]),
        pltpu.make_async_copy(mix_in, mix.at[0], w_sem.at[1]),
        pltpu.make_async_copy(wo_in, wo, w_sem.at[2]),
    ]

    barrier = pltpu.get_barrier_semaphore()
    for axis in range(3):
        for d in range(1, RING):
            pl.semaphore_signal(barrier, inc=1, device_id=(along(axis, d), h), device_id_type=MESH)
    pl.semaphore_signal(barrier, inc=1, device_id=(tm, 1 - h), device_id_type=MESH)

    for s in range(count):
        load_x(s).start()
    for load in loads:
        load.start()

    rows = 256
    steps = x.shape[1]
    blocks = steps // 128
    first = tm * steps
    mode_high = jnp.broadcast_to((modes[...] >> 7).astype(F32), (128, 128)).astype(BF16)
    mode_low = jnp.broadcast_to((modes[...] & 127).astype(F32), (128, 128)).astype(BF16)
    pick = one_hot((rows, 128), iota((rows, 128), 0) // 2)
    by_row = (dot_nt(pick, mode_high) * 128.0 + dot_nt(pick, mode_low)).astype(jnp.int32)
    quarter_turn = (iota((rows, 128), 0) & 1) * (PERIOD // 4)
    cos_low, sin_low = cos_sin(by_row * iota((rows, 128), 1))
    cos_high, sin_high = cos_sin(
        by_row * (first + 128 * (iota((rows, 128), 1) & (blocks - 1))) + quarter_turn
    )
    for i in range(blocks):
        value = cos_high[:, i : i + 1] * cos_low - sin_high[:, i : i + 1] * sin_low
        table[0, :, pl.ds(128 * i, 128)] = value.astype(BF16)
    for part in range(1, PARTS):
        perm = one_hot((rows, rows), order_row(iota((rows, rows), 0), part))
        table[part] = dot(perm, table[0]).astype(BF16)

    pl.semaphore_wait(barrier, 10)
    to_partner(wq_in, wq.at[1], 0).start()
    to_partner(mix_in, mix.at[1], 1).start()

    def band(axis, d):
        c = lax.rem(coord(axis) + d, RING)
        return pl.ds(pl.multiple_of(c * 64, 64), 64)

    def stage1(s, way, kind):
        axis = lax.rem(s, PARTS)
        near = 1 if way == 0 else 3
        mine = pl.ds(256 * way, 256)
        other = pl.ds(256 * (1 - way), 256)
        slot = 2 * kind + way
        if kind == 0:
            src, dst = sent.at[s, band(axis, 2), mine], ra.at[s, way]
        elif kind == 1:
            src, dst = sent.at[s, band(axis, near), other], rb.at[s, way, :, other]
        else:
            src, dst = acc.at[s, way], rb.at[s, way, :, mine]
        return remote(src, dst, send1.at[s, slot], recv1.at[s, slot], along(axis, near))

    def forward(s, carry):
        load_x(s).wait()
        sent[s] = dot(table[lax.rem(s, PARTS)], x[s]).astype(BF16)
        for kind in range(2):
            for way in range(2):
                stage1(s, way, kind).start()
        return carry

    lax.fori_loop(0, count, forward, 0)

    def relay(s, carry):
        axis = lax.rem(s, PARTS)
        for way in range(2):
            stage1(s, way, 0).wait_recv()
            own = sent[s, band(axis, 1 if way == 0 else 3), pl.ds(256 * way, 256)]
            acc[s, way] = (own.astype(F32) + ra[s, way].astype(F32)).astype(BF16)
            stage1(s, way, 2).start()
        return carry

    lax.fori_loop(0, count, relay, 0)

    by_lane = (
        dot_nt(mode_high[0:8], pick) * 128.0 + dot_nt(mode_low[0:8], pick)
    ).astype(jnp.int32)
    turn_lane = (iota((8, rows), 1) & 1) * (PERIOD // 4)
    wide_cos, wide_sin = cos_sin(jnp.broadcast_to(by_lane[0:1], (128, rows)) * iota((128, rows), 0))
    top_cos, top_sin = cos_sin(by_lane * (first + 128 * (iota((8, rows), 0) & (blocks - 1))) + turn_lane)
    for i in range(blocks):
        value = top_cos[i : i + 1] * wide_cos - top_sin[i : i + 1] * wide_sin
        wide[0, pl.ds(128 * i, 128), :] = value.astype(BF16)
    for part in range(1, PARTS):
        perm = one_hot((rows, rows), order_row(iota((rows, rows), 0), part))
        wide[part] = dot_nt(wide[0], perm).astype(BF16)
    table_copy = pltpu.make_async_copy(wide, tab_out, o_sem.at[0])
    table_copy.start()

    for load in loads:
        load.wait()
    to_partner(wq_in, wq.at[1], 0).wait_recv()
    to_partner(mix_in, mix.at[1], 1).wait_recv()
    mw[...] = jnp.zeros_like(mw)
    left = iota((64, 128), 1) < 64
    for half in range(2):
        for m in range(2):
            for head in range(4):
                both = mix[half, m, head]
                turned = pltpu.roll(both, 64, 1)
                for kind in range(2):
                    value = both if kind == head % 2 else turned
                    keep = left if head % 2 == 0 else jnp.logical_not(left)
                    value = jnp.where(keep, value, 0.0).astype(BF16)
                    mw[half, pl.ds((2 * m + kind) * 256 + 64 * head, 64), pl.ds(128 * (head // 2), 128)] = value
    v3[...] = jnp.zeros_like(v3)

    def stage2(s, d):
        axis = lax.rem(s + 1, PARTS)
        c = lax.rem(coord(axis) + d, RING)
        return remote(
            s2.at[s, pl.ds(pl.multiple_of(c * 16, 16), 16), :], r2.at[s, d - 1],
            send2.at[s, d - 1], recv2.at[s, d - 1], along(axis, d),
        )

    def reduce1(s, carry):
        axis = lax.rem(s, PARTS)
        for kind in range(1, 3):
            for way in range(2):
                stage1(s, way, kind).wait_recv()
        total = sent[s, band(axis, 0), :].astype(F32) + rb[s, 0].astype(F32) + rb[s, 1].astype(F32)
        s2[s] = total.astype(BF16)
        for d in range(1, RING):
            stage2(s, d).start()
        return carry

    lax.fori_loop(0, count, reduce1, 0)

    def reduce2(s, carry):
        axis = lax.rem(s + 1, PARTS)
        for d in range(1, RING):
            stage2(s, d).wait_recv()
        own = s2[s, pl.ds(pl.multiple_of(coord(axis) * 16, 16), 16), :].astype(F32)
        total = own + r2[s, 0].astype(F32) + r2[s, 1].astype(F32) + r2[s, 2].astype(F32)
        row = pl.multiple_of(lax.div(s, PARTS) * 16, 16)
        v3[lax.rem(s, PARTS), pl.ds(row, 16), :] = total.astype(BF16)
        return carry

    lax.fori_loop(0, count, reduce2, 0)

    def stage3(part, d):
        axis = (part + 2) % PARTS
        c = lax.rem(coord(axis) + d, RING)
        return remote(
            s3.at[part, c], r3.at[part, d - 1],
            send3.at[part, d - 1], recv3.at[part, d - 1], along(axis, d),
        )

    k = iota((64, 64), 0)
    swap = one_hot((64, 64), ((k // 4) % 4) * 16 + (k // 16) * 4 + k % 4)
    for part in range(PARTS):
        turned = dot(swap, v3[part]).astype(BF16)
        for c in range(RING):
            s3[part, c] = turned[16 * c : 16 * c + 16]
        for d in range(1, RING):
            stage3(part, d).start()
    for part in range(PARTS):
        for d in range(1, RING):
            stage3(part, d).wait_recv()
        own = s3[part, coord((part + 2) % PARTS)].astype(F32)
        xs[pl.ds(16 * part, 16), :] = (
            own + r3[part, 0].astype(F32) + r3[part, 1].astype(F32) + r3[part, 2].astype(F32)
        )

    lhs = jnp.concatenate(split(xs[...]), axis=0)
    held = 16 * PARTS
    odd = (iota((held, 256), 0) & 1) == 1
    second = (iota((held, 256), 0) & 2) == 2
    for half in range(2):
        q = dot(lhs, wq[half])
        q = q[:held] + q[held:]
        crossed = jnp.where(odd, pltpu.roll(q, 1, 0), -pltpu.roll(q, held - 1, 0))
        pieces = [
            jnp.where(second, 0.0, q), jnp.where(second, 0.0, crossed),
            jnp.where(second, q, 0.0), jnp.where(second, crossed, 0.0),
        ]
        mixed = jnp.zeros((2 * held, 256), F32)
        for i in range(4):
            mixed = mixed + dot(jnp.concatenate(split(pieces[i]), axis=0), mw[half, pl.ds(256 * i, 256), :])
        mixed = (mixed[:held] + mixed[held:]).astype(BF16)
        mx[h, h if half == 0 else 1 - h] = mixed
    to_partner(mx.at[h], mx.at[h], 2).start()
    to_partner(mx.at[h], mx.at[h], 2).wait_recv()

    def gather1(part, d):
        axis = (part + 2) % PARTS
        c = coord(axis)
        return remote(
            a1.at[part, c], a1.at[part, c],
            g1_send.at[part, d - 1], g1_recv.at[part, d - 1], along(axis, d),
        )

    for group in range(2):
        g = dot(mx[group, 0], wo[pl.ds(0, 256), :]) + dot(mx[group, 1], wo[pl.ds(256, 256), :])
        g = (g * scale).astype(BF16)
        for part in range(PARTS):
            a1[part, coord((part + 2) % PARTS), pl.ds(16 * group, 16), :] = g[16 * part : 16 * part + 16]
    for part in range(PARTS):
        for d in range(1, RING):
            gather1(part, d).start()

    def spot(part, second_shift, first_shift=0):
        c1 = lax.rem(coord(part) + first_shift, RING)
        c2 = lax.rem(coord((part + 1) % PARTS) + second_shift, RING)
        return pl.ds(pl.multiple_of(c1 * 64 + c2 * 16, 16), 16)

    def gather2(part, d):
        return remote(
            gb.at[part, :, :, spot(part, 0), :], gb.at[part, :, :, spot(part, 0), :],
            g2_send.at[part, d - 1], g2_recv.at[part, d - 1], along((part + 1) % PARTS, d),
        )

    k = iota((96, 128), 0)
    unswap = one_hot((96, 128), ((k // 4) % 4) * 32 + (k // 48) * 16 + ((k // 16) % 3) * 4 + k % 4)
    for part in range(PARTS):
        for d in range(1, RING):
            gather1(part, d).wait_recv()
        flat = jnp.concatenate([a1[part, c] for c in range(RING)], axis=0)
        turned = dot(unswap, flat).astype(BF16)
        for group in range(2):
            for j in range(PARTS):
                at = 48 * group + 16 * j
                gb[part, group, j, spot(part, 0), :] = turned[at : at + 16]
        for d in range(1, RING):
            gather2(part, d).start()

    def gather3(part, way, group, relayed):
        near = 1 if way == 0 else 3
        c = lax.rem(coord(part) + (RING - near if relayed else 0), RING)
        at = gb.at[part, group, :, pl.ds(pl.multiple_of(c * 64, 64), 64), :]
        slot = 2 if relayed else group
        return remote(at, at, g3_send.at[part, way, slot], g3_recv.at[part, way, slot], along(part, near))

    for part in range(PARTS):
        for d in range(1, RING):
            gather2(part, d).wait_recv()
        for turn in range(2):
            for way in range(2):
                gather3(part, way, turn if way == 0 else 1 - turn, False).start()
    for part in range(PARTS):
        for way in range(2):
            gather3(part, way, way, False).wait_recv()
            gather3(part, way, way, True).start()
    gathered = []
    for part in range(PARTS):
        for way in range(2):
            gather3(part, way, 1 - way, False).wait_recv()
        for way in range(2):
            gather3(part, way, way, True).wait_recv()
        copy = pltpu.make_async_copy(gb.at[part], gat_out.at[part], o_sem.at[1 + part])
        copy.start()
        gathered.append(copy)

    def drain(s, carry):
        for kind in range(3):
            for way in range(2):
                stage1(s, way, kind).wait_send()
        for d in range(1, RING):
            stage2(s, d).wait_send()
        return carry

    lax.fori_loop(0, count, drain, 0)
    to_partner(wq_in, wq.at[1], 0).wait_send()
    to_partner(mix_in, mix.at[1], 1).wait_send()
    to_partner(mx.at[h], mx.at[h], 2).wait_send()
    for part in range(PARTS):
        for d in range(1, RING):
            stage3(part, d).wait_send()
            gather1(part, d).wait_send()
            gather2(part, d).wait_send()
        for way in range(2):
            gather3(part, way, 0, False).wait_send()
            gather3(part, way, 1, False).wait_send()
            gather3(part, way, way, True).wait_send()
    table_copy.wait()
    for copy in gathered:
        copy.wait()


def inverse_kernel(table, gathered, out):
    out[...] = dot(table[...], gathered[...]).astype(BF16)


def place(step):
    part = step // 6
    depth = 3 - part // 2
    left = step % 6
    return part, left // depth, left % depth


def body(series, modes, query_weight, mix_weight, out_weight):
    series_count, steps, width = series.shape
    group = query_weight.shape[1]
    count = series_count // 2
    scale = 1.0 / math.sqrt(PERIOD) / math.sqrt(modes.shape[0])
    any_space = pl.BlockSpec(memory_space=pl.ANY)
    dma = pltpu.SemaphoreType.DMA
    vm = pltpu.VMEM
    tables, gathered = pl.pallas_call(
        functools.partial(exchange_kernel, scale),
        out_shape=(
            jax.ShapeDtypeStruct((PARTS, steps, 256), BF16),
            jax.ShapeDtypeStruct((PARTS, 2, 3, 256, group), BF16),
        ),
        in_specs=[any_space, pl.BlockSpec(memory_space=pltpu.VMEM), any_space, any_space, any_space],
        out_specs=(any_space, any_space),
        scratch_shapes=[
            vm((count, steps, width), BF16),
            vm((PARTS, 256, steps), BF16),
            vm((PARTS, steps, 256), BF16),
            vm((count, 256, width), BF16),
            vm((count, 2, 64, 256), BF16),
            vm((count, 2, 64, width), BF16),
            vm((count, 2, 64, 256), BF16),
            vm((count, 64, width), BF16),
            vm((count, 3, 16, width), BF16),
            vm((PARTS, 64, width), BF16),
            vm((PARTS, RING, 16, width), BF16),
            vm((PARTS, 3, 16, width), BF16),
            vm((48, width), F32),
            vm((2, width, group), BF16),
            vm((2,) + mix_weight.shape, F32),
            vm((width, group), BF16),
            vm((2, 1024, 256), BF16),
            vm((2, 2, 48, 256), BF16),
            vm((PARTS, RING, 32, group), BF16),
            vm((PARTS, 2, 3, 256, group), BF16),
            dma((count,)), dma((3,)), dma((4,)), dma((3,)), dma((3,)),
            dma((count, 6)), dma((count, 6)), dma((count, 3)), dma((count, 3)),
            dma((PARTS, 3)), dma((PARTS, 3)),
            dma((PARTS, 3)), dma((PARTS, 3)), dma((PARTS, 3)), dma((PARTS, 3)),
            dma((PARTS, 2, 3)), dma((PARTS, 2, 3)),
        ],
        compiler_params=pltpu.CompilerParams(
            collective_id=0, has_side_effects=True, vmem_limit_bytes=60 * 1024 * 1024
        ),
        name="exchange",
    )(series, modes.reshape(1, -1), query_weight, mix_weight, out_weight)

    return pl.pallas_call(
        inverse_kernel,
        grid=(series_count,),
        out_shape=jax.ShapeDtypeStruct((series_count, steps, group), BF16),
        in_specs=[
            pl.BlockSpec((None, steps, 256), lambda i: (place(i)[0], 0, 0)),
            pl.BlockSpec((None, None, None, 256, group), lambda i: place(i) + (0, 0)),
        ],
        out_specs=pl.BlockSpec(
            (None, steps, group), lambda i: (place(i)[1] * 8 + 3 * place(i)[2] + place(i)[0], 0, 0)
        ),
        name="inverse",
    )(tables, gathered)


def solution(mesh):
    in_specs = (
        P(None, "tm", None),
        P(),
        P(None, "head"),
        P("tm", "head", None, None),
        P(None, "head"),
    )
    out_specs = P(None, "tm", "head")
    return jax.shard_map(body, mesh=mesh, in_specs=in_specs, out_specs=out_specs, check_vma=False)
```

```python
import functools
import math

import jax
import jax.numpy as jnp
from jax import lax
from jax.experimental import pallas as pl
from jax.experimental.pallas import tpu as pltpu
from jax.sharding import PartitionSpec as P

F32 = jnp.float32
BF16 = jnp.bfloat16
MESH = pl.DeviceIdType.MESH
RING = 4
PARTS = 3
PERIOD = 65536


def iota(shape, dim):
    return lax.broadcasted_iota(jnp.int32, shape, dim)


def one_hot(shape, wanted):
    return (iota(shape, 1) == wanted).astype(F32).astype(BF16)


def dot(a, b):
    return jnp.dot(a, b, preferred_element_type=F32)


def dot_nt(a, b):
    return lax.dot_general(a, b, (((1,), (1,)), ((), ())), preferred_element_type=F32)


def cos_sin(phase):
    phase = phase & (PERIOD - 1)
    quarter = (phase + PERIOD // 8) >> 14
    r = (phase - (quarter << 14)).astype(F32) * (2.0 * math.pi / PERIOD)
    q = r * r
    s = r * (1.0 + q * (-1 / 6 + q * (1 / 120 + q * (-1 / 5040 + q * (1 / 362880)))))
    c = 1.0 + q * (-0.5 + q * (1 / 24 + q * (-1 / 720 + q * (1 / 40320))))
    odd = (quarter & 1) == 1
    cos_value = jnp.where(odd, s, c)
    sin_value = jnp.where(odd, c, s)
    cos_value = jnp.where(((quarter + 1) & 2) != 0, -cos_value, cos_value)
    sin_value = jnp.where((quarter & 2) != 0, -sin_value, sin_value)
    return cos_value, sin_value


def stride_of(axis):
    return 16 - 12 * axis + 9 * ((axis * (axis - 1)) // 2)


def split(x):
    high = x.astype(BF16)
    low = (x - high.astype(F32)).astype(BF16)
    return high, low


def order_row(k, part):
    first, second, third, r = k // 64, (k // 16) % 4, (k // 4) % 4, k % 4
    if part == 0:
        return k
    if part == 1:
        return third * 64 + first * 16 + second * 4 + r
    return second * 64 + third * 16 + first * 4 + r


def exchange_kernel(
    scale, series, modes, wq_in, mix_in, wo_in, tab_out, gat_out,
    x, table, wide, sent, ra, rb, acc, s2, r2, v3, s3, r3, xs, wq, mix, wo, mw, mx, a1, gb,
    x_sem, w_sem, o_sem, p_send, p_recv, send1, recv1, send2, recv2, send3, recv3,
    g1_send, g1_recv, g2_send, g2_recv, g3_send, g3_recv,
):
    tm = lax.axis_index("tm")
    h = lax.axis_index("head")
    count = x.shape[0]

    def coord(axis):
        return lax.rem(lax.div(tm, stride_of(axis)), RING)

    def along(axis, distance):
        c = coord(axis)
        return tm + (lax.rem(c + distance, RING) - c) * stride_of(axis)

    def remote(src, dst, ssem, rsem, target):
        return pltpu.make_async_remote_copy(
            src_ref=src, dst_ref=dst, send_sem=ssem, recv_sem=rsem,
            device_id=(target, h), device_id_type=MESH,
        )

    def to_partner(src, dst, k):
        return pltpu.make_async_remote_copy(
            src_ref=src, dst_ref=dst, send_sem=p_send.at[k], recv_sem=p_recv.at[k],
            device_id=(tm, 1 - h), device_id_type=MESH,
        )

    def load_x(s):
        return pltpu.make_async_copy(series.at[h * count + s], x.at[s], x_sem.at[s])

    loads = [
        pltpu.make_async_copy(wq_in, wq.at[0], w_sem.at[0]),
        pltpu.make_async_copy(mix_in, mix.at[0], w_sem.at[1]),
        pltpu.make_async_copy(wo_in, wo, w_sem.at[2]),
    ]

    barrier = pltpu.get_barrier_semaphore()
    for axis in range(3):
        for d in range(1, RING):
            pl.semaphore_signal(barrier, inc=1, device_id=(along(axis, d), h), device_id_type=MESH)
    pl.semaphore_signal(barrier, inc=1, device_id=(tm, 1 - h), device_id_type=MESH)

    for s in range(count):
        load_x(s).start()
    for load in loads:
        load.start()

    rows = 256
    steps = x.shape[1]
    blocks = steps // 128
    first = tm * steps
    mode_high = jnp.broadcast_to((modes[...] >> 7).astype(F32), (128, 128)).astype(BF16)
    mode_low = jnp.broadcast_to((modes[...] & 127).astype(F32), (128, 128)).astype(BF16)
    pick = one_hot((rows, 128), iota((rows, 128), 0) // 2)
    by_row = (dot_nt(pick, mode_high) * 128.0 + dot_nt(pick, mode_low)).astype(jnp.int32)
    quarter_turn = (iota((rows, 128), 0) & 1) * (PERIOD // 4)
    cos_low, sin_low = cos_sin(by_row * iota((rows, 128), 1))
    cos_high, sin_high = cos_sin(
        by_row * (first + 128 * (iota((rows, 128), 1) & (blocks - 1))) + quarter_turn
    )
    for i in range(blocks):
        value = cos_high[:, i : i + 1] * cos_low - sin_high[:, i : i + 1] * sin_low
        table[0, :, pl.ds(128 * i, 128)] = value.astype(BF16)
    for part in range(1, PARTS):
        perm = one_hot((rows, rows), order_row(iota((rows, rows), 0), part))
        table[part] = dot(perm, table[0]).astype(BF16)

    pl.semaphore_wait(barrier, 10)
    to_partner(wq_in, wq.at[1], 0).start()
    to_partner(mix_in, mix.at[1], 1).start()

    def band(axis, d):
        c = lax.rem(coord(axis) + d, RING)
        return pl.ds(pl.multiple_of(c * 64, 64), 64)

    def stage1(s, way, kind):
        axis = lax.rem(s, PARTS)
        near = 1 if way == 0 else 3
        mine = pl.ds(256 * way, 256)
        other = pl.ds(256 * (1 - way), 256)
        slot = 2 * kind + way
        if kind == 0:
            src, dst = sent.at[s, band(axis, 2), mine], ra.at[s, way]
        elif kind == 1:
            src, dst = sent.at[s, band(axis, near), other], rb.at[s, way, :, other]
        else:
            src, dst = acc.at[s, way], rb.at[s, way, :, mine]
        return remote(src, dst, send1.at[s, slot], recv1.at[s, slot], along(axis, near))

    def forward(s, carry):
        load_x(s).wait()
        sent[s] = dot(table[lax.rem(s, PARTS)], x[s]).astype(BF16)
        for kind in range(2):
            for way in range(2):
                stage1(s, way, kind).start()
        return carry

    lax.fori_loop(0, count, forward, 0)

    def relay(s, carry):
        axis = lax.rem(s, PARTS)
        for way in range(2):
            stage1(s, way, 0).wait_recv()
            own = sent[s, band(axis, 1 if way == 0 else 3), pl.ds(256 * way, 256)]
            acc[s, way] = (own.astype(F32) + ra[s, way].astype(F32)).astype(BF16)
            stage1(s, way, 2).start()
        return carry

    lax.fori_loop(0, count, relay, 0)

    by_lane = (
        dot_nt(mode_high[0:8], pick) * 128.0 + dot_nt(mode_low[0:8], pick)
    ).astype(jnp.int32)
    turn_lane = (iota((8, rows), 1) & 1) * (PERIOD // 4)
    wide_cos, wide_sin = cos_sin(jnp.broadcast_to(by_lane[0:1], (128, rows)) * iota((128, rows), 0))
    top_cos, top_sin = cos_sin(by_lane * (first + 128 * (iota((8, rows), 0) & (blocks - 1))) + turn_lane)
    for i in range(blocks):
        value = top_cos[i : i + 1] * wide_cos - top_sin[i : i + 1] * wide_sin
        wide[0, pl.ds(128 * i, 128), :] = value.astype(BF16)
    for part in range(1, PARTS):
        perm = one_hot((rows, rows), order_row(iota((rows, rows), 0), part))
        wide[part] = dot_nt(wide[0], perm).astype(BF16)
    table_copy = pltpu.make_async_copy(wide, tab_out, o_sem.at[0])
    table_copy.start()

    for load in loads:
        load.wait()
    to_partner(wq_in, wq.at[1], 0).wait_recv()
    to_partner(mix_in, mix.at[1], 1).wait_recv()
    mw[...] = jnp.zeros_like(mw)
    left = iota((64, 128), 1) < 64
    for half in range(2):
        for m in range(2):
            for head in range(4):
                both = mix[half, m, head]
                turned = pltpu.roll(both, 64, 1)
                for kind in range(2):
                    value = both if kind == head % 2 else turned
                    keep = left if head % 2 == 0 else jnp.logical_not(left)
                    value = jnp.where(keep, value, 0.0).astype(BF16)
                    mw[half, pl.ds((2 * m + kind) * 256 + 64 * head, 64), pl.ds(128 * (head // 2), 128)] = value
    v3[...] = jnp.zeros_like(v3)

    def stage2(s, d):
        axis = lax.rem(s + 1, PARTS)
        c = lax.rem(coord(axis) + d, RING)
        return remote(
            s2.at[s, pl.ds(pl.multiple_of(c * 16, 16), 16), :], r2.at[s, d - 1],
            send2.at[s, d - 1], recv2.at[s, d - 1], along(axis, d),
        )

    def reduce1(s, carry):
        axis = lax.rem(s, PARTS)
        for kind in range(1, 3):
            for way in range(2):
                stage1(s, way, kind).wait_recv()
        total = sent[s, band(axis, 0), :].astype(F32) + rb[s, 0].astype(F32) + rb[s, 1].astype(F32)
        s2[s] = total.astype(BF16)
        for d in range(1, RING):
            stage2(s, d).start()
        return carry

    lax.fori_loop(0, count, reduce1, 0)

    def reduce2(s, carry):
        axis = lax.rem(s + 1, PARTS)
        for d in range(1, RING):
            stage2(s, d).wait_recv()
        own = s2[s, pl.ds(pl.multiple_of(coord(axis) * 16, 16), 16), :].astype(F32)
        total = own + r2[s, 0].astype(F32) + r2[s, 1].astype(F32) + r2[s, 2].astype(F32)
        row = pl.multiple_of(lax.div(s, PARTS) * 16, 16)
        v3[lax.rem(s, PARTS), pl.ds(row, 16), :] = total.astype(BF16)
        return carry

    lax.fori_loop(0, count, reduce2, 0)

    def stage3(part, d):
        axis = (part + 2) % PARTS
        c = lax.rem(coord(axis) + d, RING)
        return remote(
            s3.at[part, c], r3.at[part, d - 1],
            send3.at[part, d - 1], recv3.at[part, d - 1], along(axis, d),
        )

    k = iota((64, 64), 0)
    swap = one_hot((64, 64), ((k // 4) % 4) * 16 + (k // 16) * 4 + k % 4)
    for part in range(PARTS):
        turned = dot(swap, v3[part]).astype(BF16)
        for c in range(RING):
            s3[part, c] = turned[16 * c : 16 * c + 16]
        for d in range(1, RING):
            stage3(part, d).start()
    for part in range(PARTS):
        for d in range(1, RING):
            stage3(part, d).wait_recv()
        own = s3[part, coord((part + 2) % PARTS)].astype(F32)
        xs[pl.ds(16 * part, 16), :] = (
            own + r3[part, 0].astype(F32) + r3[part, 1].astype(F32) + r3[part, 2].astype(F32)
        )

    lhs = jnp.concatenate(split(xs[...]), axis=0)
    held = 16 * PARTS
    odd = (iota((held, 256), 0) & 1) == 1
    second = (iota((held, 256), 0) & 2) == 2
    for half in range(2):
        q = dot(lhs, wq[half])
        q = q[:held] + q[held:]
        crossed = jnp.where(odd, pltpu.roll(q, 1, 0), -pltpu.roll(q, held - 1, 0))
        pieces = [
            jnp.where(second, 0.0, q), jnp.where(second, 0.0, crossed),
            jnp.where(second, q, 0.0), jnp.where(second, crossed, 0.0),
        ]
        mixed = jnp.zeros((2 * held, 256), F32)
        for i in range(4):
            mixed = mixed + dot(jnp.concatenate(split(pieces[i]), axis=0), mw[half, pl.ds(256 * i, 256), :])
        mixed = (mixed[:held] + mixed[held:]).astype(BF16)
        mx[h, h if half == 0 else 1 - h] = mixed
    to_partner(mx.at[h], mx.at[h], 2).start()
    to_partner(mx.at[h], mx.at[h], 2).wait_recv()

    def gather1(part, d):
        axis = (part + 2) % PARTS
        c = coord(axis)
        return remote(
            a1.at[part, c], a1.at[part, c],
            g1_send.at[part, d - 1], g1_recv.at[part, d - 1], along(axis, d),
        )

    for group in range(2):
        g = dot(mx[group, 0], wo[pl.ds(0, 256), :]) + dot(mx[group, 1], wo[pl.ds(256, 256), :])
        g = (g * scale).astype(BF16)
        for part in range(PARTS):
            a1[part, coord((part + 2) % PARTS), pl.ds(16 * group, 16), :] = g[16 * part : 16 * part + 16]
    for part in range(PARTS):
        for d in range(1, RING):
            gather1(part, d).start()

    def spot(part, second_shift, first_shift=0):
        c1 = lax.rem(coord(part) + first_shift, RING)
        c2 = lax.rem(coord((part + 1) % PARTS) + second_shift, RING)
        return pl.ds(pl.multiple_of(c1 * 64 + c2 * 16, 16), 16)

    def gather2(part, d):
        return remote(
            gb.at[part, :, :, spot(part, 0), :], gb.at[part, :, :, spot(part, 0), :],
            g2_send.at[part, d - 1], g2_recv.at[part, d - 1], along((part + 1) % PARTS, d),
        )

    k = iota((96, 128), 0)
    unswap = one_hot((96, 128), ((k // 4) % 4) * 32 + (k // 48) * 16 + ((k // 16) % 3) * 4 + k % 4)
    for part in range(PARTS):
        for d in range(1, RING):
            gather1(part, d).wait_recv()
        flat = jnp.concatenate([a1[part, c] for c in range(RING)], axis=0)
        turned = dot(unswap, flat).astype(BF16)
        for group in range(2):
            for j in range(PARTS):
                at = 48 * group + 16 * j
                gb[part, group, j, spot(part, 0), :] = turned[at : at + 16]
        for d in range(1, RING):
            gather2(part, d).start()

    def gather3(part, way, group, relayed):
        near = 1 if way == 0 else 3
        c = lax.rem(coord(part) + (RING - near if relayed else 0), RING)
        at = gb.at[part, group, :, pl.ds(pl.multiple_of(c * 64, 64), 64), :]
        slot = 2 if relayed else group
        return remote(at, at, g3_send.at[part, way, slot], g3_recv.at[part, way, slot], along(part, near))

    for part in range(PARTS):
        for d in range(1, RING):
            gather2(part, d).wait_recv()
        for turn in range(2):
            for way in range(2):
                gather3(part, way, turn if way == 0 else 1 - turn, False).start()
    for part in range(PARTS):
        for way in range(2):
            gather3(part, way, way, False).wait_recv()
            gather3(part, way, way, True).start()
    gathered = []
    for part in range(PARTS):
        for way in range(2):
            gather3(part, way, 1 - way, False).wait_recv()
        for way in range(2):
            gather3(part, way, way, True).wait_recv()
        copy = pltpu.make_async_copy(gb.at[part], gat_out.at[part], o_sem.at[1 + part])
        copy.start()
        gathered.append(copy)

    def drain(s, carry):
        for kind in range(3):
            for way in range(2):
                stage1(s, way, kind).wait_send()
        for d in range(1, RING):
            stage2(s, d).wait_send()
        return carry

    lax.fori_loop(0, count, drain, 0)
    to_partner(wq_in, wq.at[1], 0).wait_send()
    to_partner(mix_in, mix.at[1], 1).wait_send()
    to_partner(mx.at[h], mx.at[h], 2).wait_send()
    for part in range(PARTS):
        for d in range(1, RING):
            stage3(part, d).wait_send()
            gather1(part, d).wait_send()
            gather2(part, d).wait_send()
        for way in range(2):
            gather3(part, way, 0, False).wait_send()
            gather3(part, way, 1, False).wait_send()
            gather3(part, way, way, True).wait_send()
    table_copy.wait()
    for copy in gathered:
        copy.wait()


def inverse_kernel(tab_in, gat_in, out, tab, gat, res, t_sem, g_sem, o_sem):
    def load_tab(part):
        return pltpu.make_async_copy(tab_in.at[part], tab.at[part], t_sem.at[part])

    def load_gat(part):
        return pltpu.make_async_copy(gat_in.at[part], gat.at[part], g_sem.at[part])

    def store(s):
        return pltpu.make_async_copy(res.at[s], out.at[s], o_sem.at[s])

    for part in range(PARTS):
        load_tab(part).start()
        load_gat(part).start()
    for part in range(PARTS):
        load_tab(part).wait()
        load_gat(part).wait()

        def step(j, carry):
            for group in range(2):
                s = 8 * group + 3 * j + part
                res[s] = dot(tab[part], gat[part, group, j]).astype(BF16)
                store(s).start()
            return carry

        lax.fori_loop(0, 3 - part // 2, step, 0)

    def drain(s, carry):
        store(s).wait()
        return carry

    lax.fori_loop(0, out.shape[0], drain, 0)


def body(series, modes, query_weight, mix_weight, out_weight):
    series_count, steps, width = series.shape
    group = query_weight.shape[1]
    count = series_count // 2
    scale = 1.0 / math.sqrt(PERIOD) / math.sqrt(modes.shape[0])
    any_space = pl.BlockSpec(memory_space=pl.ANY)
    dma = pltpu.SemaphoreType.DMA
    vm = pltpu.VMEM
    tables, gathered = pl.pallas_call(
        functools.partial(exchange_kernel, scale),
        out_shape=(
            jax.ShapeDtypeStruct((PARTS, steps, 256), BF16),
            jax.ShapeDtypeStruct((PARTS, 2, 3, 256, group), BF16),
        ),
        in_specs=[any_space, pl.BlockSpec(memory_space=pltpu.VMEM), any_space, any_space, any_space],
        out_specs=(any_space, any_space),
        scratch_shapes=[
            vm((count, steps, width), BF16),
            vm((PARTS, 256, steps), BF16),
            vm((PARTS, steps, 256), BF16),
            vm((count, 256, width), BF16),
            vm((count, 2, 64, 256), BF16),
            vm((count, 2, 64, width), BF16),
            vm((count, 2, 64, 256), BF16),
            vm((count, 64, width), BF16),
            vm((count, 3, 16, width), BF16),
            vm((PARTS, 64, width), BF16),
            vm((PARTS, RING, 16, width), BF16),
            vm((PARTS, 3, 16, width), BF16),
            vm((48, width), F32),
            vm((2, width, group), BF16),
            vm((2,) + mix_weight.shape, F32),
            vm((width, group), BF16),
            vm((2, 1024, 256), BF16),
            vm((2, 2, 48, 256), BF16),
            vm((PARTS, RING, 32, group), BF16),
            vm((PARTS, 2, 3, 256, group), BF16),
            dma((count,)), dma((3,)), dma((4,)), dma((3,)), dma((3,)),
            dma((count, 6)), dma((count, 6)), dma((count, 3)), dma((count, 3)),
            dma((PARTS, 3)), dma((PARTS, 3)),
            dma((PARTS, 3)), dma((PARTS, 3)), dma((PARTS, 3)), dma((PARTS, 3)),
            dma((PARTS, 2, 3)), dma((PARTS, 2, 3)),
        ],
        compiler_params=pltpu.CompilerParams(
            collective_id=0, has_side_effects=True, vmem_limit_bytes=60 * 1024 * 1024
        ),
        name="exchange",
    )(series, modes.reshape(1, -1), query_weight, mix_weight, out_weight)

    return pl.pallas_call(
        inverse_kernel,
        out_shape=jax.ShapeDtypeStruct((series_count, steps, group), BF16),
        in_specs=[any_space, any_space],
        out_specs=any_space,
        scratch_shapes=[
            vm((PARTS, steps, 256), BF16),
            vm((PARTS, 2, 3, 256, group), BF16),
            vm((series_count, steps, group), BF16),
            dma((PARTS,)), dma((PARTS,)), dma((series_count,)),
        ],
        compiler_params=pltpu.CompilerParams(vmem_limit_bytes=60 * 1024 * 1024),
        name="inverse",
    )(tables, gathered)


def solution(mesh):
    in_specs = (
        P(None, "tm", None),
        P(),
        P(None, "head"),
        P("tm", "head", None, None),
        P(None, "head"),
    )
    out_specs = P(None, "tm", "head")
    return jax.shard_map(body, mesh=mesh, in_specs=in_specs, out_specs=out_specs, check_vma=False)
```

```python
import functools
import math

import jax
import jax.numpy as jnp
from jax import lax
from jax.experimental import pallas as pl
from jax.experimental.pallas import tpu as pltpu
from jax.sharding import PartitionSpec as P

F32 = jnp.float32
BF16 = jnp.bfloat16
MESH = pl.DeviceIdType.MESH
RING = 4
PARTS = 3
PERIOD = 65536


def iota(shape, dim):
    return lax.broadcasted_iota(jnp.int32, shape, dim)


def one_hot(shape, wanted):
    return (iota(shape, 1) == wanted).astype(F32).astype(BF16)


def dot(a, b):
    return jnp.dot(a, b, preferred_element_type=F32)


def dot_nt(a, b):
    return lax.dot_general(a, b, (((1,), (1,)), ((), ())), preferred_element_type=F32)


def cos_sin(phase):
    phase = phase & (PERIOD - 1)
    quarter = (phase + PERIOD // 8) >> 14
    r = (phase - (quarter << 14)).astype(F32) * (2.0 * math.pi / PERIOD)
    q = r * r
    s = r * (1.0 + q * (-1 / 6 + q * (1 / 120 + q * (-1 / 5040 + q * (1 / 362880)))))
    c = 1.0 + q * (-0.5 + q * (1 / 24 + q * (-1 / 720 + q * (1 / 40320))))
    odd = (quarter & 1) == 1
    cos_value = jnp.where(odd, s, c)
    sin_value = jnp.where(odd, c, s)
    cos_value = jnp.where(((quarter + 1) & 2) != 0, -cos_value, cos_value)
    sin_value = jnp.where((quarter & 2) != 0, -sin_value, sin_value)
    return cos_value, sin_value


def stride_of(axis):
    return 16 - 12 * axis + 9 * ((axis * (axis - 1)) // 2)


def split(x):
    high = x.astype(BF16)
    low = (x - high.astype(F32)).astype(BF16)
    return high, low


def order_row(k, part):
    first, second, third, r = k // 64, (k // 16) % 4, (k // 4) % 4, k % 4
    if part == 0:
        return k
    if part == 1:
        return third * 64 + first * 16 + second * 4 + r
    return second * 64 + third * 16 + first * 4 + r


def exchange_kernel(
    scale, series, modes, wq_in, mix_in, wo_in, tab_out, gat_out,
    x, table, wide, sent, ra, rb, acc, s2, r2, v3, s3, r3, xs, wq, mix, wo, mw, mx, a1, gb,
    x_sem, w_sem, o_sem, p_send, p_recv, send1, recv1, send2, recv2, send3, recv3,
    g1_send, g1_recv, g2_send, g2_recv, g3_send, g3_recv,
):
    tm = lax.axis_index("tm")
    h = lax.axis_index("head")
    count = x.shape[0]

    def coord(axis):
        return lax.rem(lax.div(tm, stride_of(axis)), RING)

    def along(axis, distance):
        c = coord(axis)
        return tm + (lax.rem(c + distance, RING) - c) * stride_of(axis)

    def remote(src, dst, ssem, rsem, target):
        return pltpu.make_async_remote_copy(
            src_ref=src, dst_ref=dst, send_sem=ssem, recv_sem=rsem,
            device_id=(target, h), device_id_type=MESH,
        )

    def to_partner(src, dst, k):
        return pltpu.make_async_remote_copy(
            src_ref=src, dst_ref=dst, send_sem=p_send.at[k], recv_sem=p_recv.at[k],
            device_id=(tm, 1 - h), device_id_type=MESH,
        )

    def load_x(s):
        return pltpu.make_async_copy(series.at[h * count + s], x.at[s], x_sem.at[s])

    loads = [
        pltpu.make_async_copy(wq_in, wq.at[0], w_sem.at[0]),
        pltpu.make_async_copy(mix_in, mix.at[0], w_sem.at[1]),
        pltpu.make_async_copy(wo_in, wo, w_sem.at[2]),
    ]

    barrier = pltpu.get_barrier_semaphore()
    for axis in range(3):
        for d in range(1, RING):
            pl.semaphore_signal(barrier, inc=1, device_id=(along(axis, d), h), device_id_type=MESH)
    pl.semaphore_signal(barrier, inc=1, device_id=(tm, 1 - h), device_id_type=MESH)

    for s in range(count):
        load_x(s).start()
    for load in loads:
        load.start()

    rows = 256
    steps = x.shape[1]
    blocks = steps // 128
    first = tm * steps
    mode_high = jnp.broadcast_to((modes[...] >> 7).astype(F32), (128, 128)).astype(BF16)
    mode_low = jnp.broadcast_to((modes[...] & 127).astype(F32), (128, 128)).astype(BF16)
    pick = one_hot((rows, 128), iota((rows, 128), 0) // 2)
    by_row = (dot_nt(pick, mode_high) * 128.0 + dot_nt(pick, mode_low)).astype(jnp.int32)
    quarter_turn = (iota((rows, 128), 0) & 1) * (PERIOD // 4)
    cos_low, sin_low = cos_sin(by_row * iota((rows, 128), 1))
    cos_high, sin_high = cos_sin(
        by_row * (first + 128 * (iota((rows, 128), 1) & (blocks - 1))) + quarter_turn
    )
    for i in range(blocks):
        value = cos_high[:, i : i + 1] * cos_low - sin_high[:, i : i + 1] * sin_low
        table[0, :, pl.ds(128 * i, 128)] = value.astype(BF16)
    for part in range(1, PARTS):
        perm = one_hot((rows, rows), order_row(iota((rows, rows), 0), part))
        table[part] = dot(perm, table[0]).astype(BF16)

    pl.semaphore_wait(barrier, 10)
    to_partner(wq_in, wq.at[1], 0).start()
    to_partner(mix_in, mix.at[1], 1).start()

    def band(axis, d):
        c = lax.rem(coord(axis) + d, RING)
        return pl.ds(pl.multiple_of(c * 64, 64), 64)

    def stage1(s, way, kind):
        axis = lax.rem(s, PARTS)
        near = 1 if way == 0 else 3
        mine = pl.ds(256 * way, 256)
        other = pl.ds(256 * (1 - way), 256)
        slot = 2 * kind + way
        if kind == 0:
            src, dst = sent.at[s, band(axis, 2), mine], ra.at[s, way]
        elif kind == 1:
            src, dst = sent.at[s, band(axis, near), other], rb.at[s, way, :, other]
        else:
            src, dst = acc.at[s, way], rb.at[s, way, :, mine]
        return remote(src, dst, send1.at[s, slot], recv1.at[s, slot], along(axis, near))

    def forward(s, carry):
        load_x(s).wait()
        sent[s] = dot(table[lax.rem(s, PARTS)], x[s]).astype(BF16)
        for kind in range(2):
            for way in range(2):
                stage1(s, way, kind).start()
        return carry

    lax.fori_loop(0, count, forward, 0)

    def relay(s, carry):
        axis = lax.rem(s, PARTS)
        for way in range(2):
            stage1(s, way, 0).wait_recv()
            own = sent[s, band(axis, 1 if way == 0 else 3), pl.ds(256 * way, 256)]
            acc[s, way] = (own.astype(F32) + ra[s, way].astype(F32)).astype(BF16)
            stage1(s, way, 2).start()
        return carry

    lax.fori_loop(0, count, relay, 0)

    by_lane = (
        dot_nt(mode_high[0:8], pick) * 128.0 + dot_nt(mode_low[0:8], pick)
    ).astype(jnp.int32)
    turn_lane = (iota((8, rows), 1) & 1) * (PERIOD // 4)
    wide_cos, wide_sin = cos_sin(jnp.broadcast_to(by_lane[0:1], (128, rows)) * iota((128, rows), 0))
    top_cos, top_sin = cos_sin(by_lane * (first + 128 * (iota((8, rows), 0) & (blocks - 1))) + turn_lane)
    for i in range(blocks):
        value = top_cos[i : i + 1] * wide_cos - top_sin[i : i + 1] * wide_sin
        wide[0, pl.ds(128 * i, 128), :] = value.astype(BF16)
    for part in range(1, PARTS):
        perm = one_hot((rows, rows), order_row(iota((rows, rows), 0), part))
        wide[part] = dot_nt(wide[0], perm).astype(BF16)
    table_copy = pltpu.make_async_copy(wide, tab_out, o_sem.at[0])
    table_copy.start()

    for load in loads:
        load.wait()
    to_partner(wq_in, wq.at[1], 0).wait_recv()
    to_partner(mix_in, mix.at[1], 1).wait_recv()
    mw[...] = jnp.zeros_like(mw)
    left = iota((64, 128), 1) < 64
    for half in range(2):
        for m in range(2):
            for head in range(4):
                both = mix[half, m, head]
                turned = pltpu.roll(both, 64, 1)
                for kind in range(2):
                    value = both if kind == head % 2 else turned
                    keep = left if head % 2 == 0 else jnp.logical_not(left)
                    value = jnp.where(keep, value, 0.0).astype(BF16)
                    mw[half, pl.ds((2 * m + kind) * 256 + 64 * head, 64), pl.ds(128 * (head // 2), 128)] = value
    v3[...] = jnp.zeros_like(v3)

    def stage2(s, d):
        axis = lax.rem(s + 1, PARTS)
        c = lax.rem(coord(axis) + d, RING)
        return remote(
            s2.at[s, pl.ds(pl.multiple_of(c * 16, 16), 16), :], r2.at[s, d - 1],
            send2.at[s, d - 1], recv2.at[s, d - 1], along(axis, d),
        )

    def reduce1(s, carry):
        axis = lax.rem(s, PARTS)
        for kind in range(1, 3):
            for way in range(2):
                stage1(s, way, kind).wait_recv()
        total = sent[s, band(axis, 0), :].astype(F32) + rb[s, 0].astype(F32) + rb[s, 1].astype(F32)
        s2[s] = total.astype(BF16)
        for d in range(1, RING):
            stage2(s, d).start()
        return carry

    lax.fori_loop(0, count, reduce1, 0)

    def reduce2(s, carry):
        axis = lax.rem(s + 1, PARTS)
        for d in range(1, RING):
            stage2(s, d).wait_recv()
        own = s2[s, pl.ds(pl.multiple_of(coord(axis) * 16, 16), 16), :].astype(F32)
        total = own + r2[s, 0].astype(F32) + r2[s, 1].astype(F32) + r2[s, 2].astype(F32)
        row = pl.multiple_of(lax.div(s, PARTS) * 16, 16)
        v3[lax.rem(s, PARTS), pl.ds(row, 16), :] = total.astype(BF16)
        return carry

    lax.fori_loop(0, count, reduce2, 0)

    def stage3(part, d):
        axis = (part + 2) % PARTS
        c = lax.rem(coord(axis) + d, RING)
        return remote(
            s3.at[part, c], r3.at[part, d - 1],
            send3.at[part, d - 1], recv3.at[part, d - 1], along(axis, d),
        )

    k = iota((64, 64), 0)
    swap = one_hot((64, 64), ((k // 4) % 4) * 16 + (k // 16) * 4 + k % 4)
    for part in range(PARTS):
        turned = dot(swap, v3[part]).astype(BF16)
        for c in range(RING):
            s3[part, c] = turned[16 * c : 16 * c + 16]
        for d in range(1, RING):
            stage3(part, d).start()
    for part in range(PARTS):
        for d in range(1, RING):
            stage3(part, d).wait_recv()
        own = s3[part, coord((part + 2) % PARTS)].astype(F32)
        xs[pl.ds(16 * part, 16), :] = (
            own + r3[part, 0].astype(F32) + r3[part, 1].astype(F32) + r3[part, 2].astype(F32)
        )

    lhs = jnp.concatenate(split(xs[...]), axis=0)
    held = 16 * PARTS
    odd = (iota((held, 256), 0) & 1) == 1
    second = (iota((held, 256), 0) & 2) == 2
    for half in range(2):
        q = dot(lhs, wq[half])
        q = q[:held] + q[held:]
        crossed = jnp.where(odd, pltpu.roll(q, 1, 0), -pltpu.roll(q, held - 1, 0))
        pieces = [
            jnp.where(second, 0.0, q), jnp.where(second, 0.0, crossed),
            jnp.where(second, q, 0.0), jnp.where(second, crossed, 0.0),
        ]
        mixed = jnp.zeros((2 * held, 256), F32)
        for i in range(4):
            mixed = mixed + dot(jnp.concatenate(split(pieces[i]), axis=0), mw[half, pl.ds(256 * i, 256), :])
        mixed = (mixed[:held] + mixed[held:]).astype(BF16)
        mx[h, h if half == 0 else 1 - h] = mixed
    to_partner(mx.at[h], mx.at[h], 2).start()
    to_partner(mx.at[h], mx.at[h], 2).wait_recv()

    def gather1(part, d):
        axis = (part + 2) % PARTS
        c = coord(axis)
        return remote(
            a1.at[part, c], a1.at[part, c],
            g1_send.at[part, d - 1], g1_recv.at[part, d - 1], along(axis, d),
        )

    for group in range(2):
        g = dot(mx[group, 0], wo[pl.ds(0, 256), :]) + dot(mx[group, 1], wo[pl.ds(256, 256), :])
        g = (g * scale).astype(BF16)
        for part in range(PARTS):
            a1[part, coord((part + 2) % PARTS), pl.ds(16 * group, 16), :] = g[16 * part : 16 * part + 16]
    for part in range(PARTS):
        for d in range(1, RING):
            gather1(part, d).start()

    def spot(part, second_shift, first_shift=0):
        c1 = lax.rem(coord(part) + first_shift, RING)
        c2 = lax.rem(coord((part + 1) % PARTS) + second_shift, RING)
        return pl.ds(pl.multiple_of(c1 * 64 + c2 * 16, 16), 16)

    def gather2(part, d):
        return remote(
            gb.at[part, :, :, spot(part, 0), :], gb.at[part, :, :, spot(part, 0), :],
            g2_send.at[part, d - 1], g2_recv.at[part, d - 1], along((part + 1) % PARTS, d),
        )

    def gather3(part, way, piece, relayed):
        near = 1 if way == 0 else 3
        if relayed:
            at = gb.at[part, way, :, spot(part, piece, RING - near), :]
        else:
            at = gb.at[part, :, :, spot(part, piece), :]
        slot = piece + (RING if relayed else 0)
        return remote(at, at, g3_send.at[part, way, slot], g3_recv.at[part, way, slot], along(part, near))

    k = iota((96, 128), 0)
    unswap = one_hot((96, 128), ((k // 4) % 4) * 32 + (k // 48) * 16 + ((k // 16) % 3) * 4 + k % 4)
    for part in range(PARTS):
        for d in range(1, RING):
            gather1(part, d).wait_recv()
        flat = jnp.concatenate([a1[part, c] for c in range(RING)], axis=0)
        turned = dot(unswap, flat).astype(BF16)
        for group in range(2):
            for j in range(PARTS):
                at = 48 * group + 16 * j
                gb[part, group, j, spot(part, 0), :] = turned[at : at + 16]
        for d in range(1, RING):
            gather2(part, d).start()
        for way in range(2):
            gather3(part, way, 0, False).start()

    def relay3(piece):
        for part in range(PARTS):
            for way in range(2):
                gather3(part, way, piece, False).wait_recv()
                gather3(part, way, piece, True).start()

    relayed = 0
    for d in (1, 3, 2):
        for part in range(PARTS):
            gather2(part, d).wait_recv()
            for way in range(2):
                gather3(part, way, RING - d, False).start()
        relay3(relayed)
        relayed = RING - d
    relay3(relayed)
    gathered = []
    for part in range(PARTS):
        for way in range(2):
            for piece in range(RING):
                gather3(part, way, piece, True).wait_recv()
        copy = pltpu.make_async_copy(gb.at[part], gat_out.at[part], o_sem.at[1 + part])
        copy.start()
        gathered.append(copy)

    def drain(s, carry):
        for kind in range(3):
            for way in range(2):
                stage1(s, way, kind).wait_send()
        for d in range(1, RING):
            stage2(s, d).wait_send()
        return carry

    lax.fori_loop(0, count, drain, 0)
    to_partner(wq_in, wq.at[1], 0).wait_send()
    to_partner(mix_in, mix.at[1], 1).wait_send()
    to_partner(mx.at[h], mx.at[h], 2).wait_send()
    for part in range(PARTS):
        for d in range(1, RING):
            stage3(part, d).wait_send()
            gather1(part, d).wait_send()
            gather2(part, d).wait_send()
        for way in range(2):
            for piece in range(RING):
                gather3(part, way, piece, False).wait_send()
                gather3(part, way, piece, True).wait_send()
    table_copy.wait()
    for copy in gathered:
        copy.wait()


def inverse_kernel(tab_in, gat_in, out, tab, gat, res, t_sem, g_sem, o_sem):
    def load_tab(part):
        return pltpu.make_async_copy(tab_in.at[part], tab.at[part], t_sem.at[part])

    def load_gat(part):
        return pltpu.make_async_copy(gat_in.at[part], gat.at[part], g_sem.at[part])

    def store(s):
        return pltpu.make_async_copy(res.at[s], out.at[s], o_sem.at[s])

    for part in range(PARTS):
        load_tab(part).start()
        load_gat(part).start()
    for part in range(PARTS):
        load_tab(part).wait()
        load_gat(part).wait()

        def step(j, carry):
            for group in range(2):
                s = 8 * group + 3 * j + part
                res[s] = dot(tab[part], gat[part, group, j]).astype(BF16)
                store(s).start()
            return carry

        lax.fori_loop(0, 3 - part // 2, step, 0)

    def drain(s, carry):
        store(s).wait()
        return carry

    lax.fori_loop(0, out.shape[0], drain, 0)


def body(series, modes, query_weight, mix_weight, out_weight):
    series_count, steps, width = series.shape
    group = query_weight.shape[1]
    count = series_count // 2
    scale = 1.0 / math.sqrt(PERIOD) / math.sqrt(modes.shape[0])
    any_space = pl.BlockSpec(memory_space=pl.ANY)
    dma = pltpu.SemaphoreType.DMA
    vm = pltpu.VMEM
    tables, gathered = pl.pallas_call(
        functools.partial(exchange_kernel, scale),
        out_shape=(
            jax.ShapeDtypeStruct((PARTS, steps, 256), BF16),
            jax.ShapeDtypeStruct((PARTS, 2, 3, 256, group), BF16),
        ),
        in_specs=[any_space, pl.BlockSpec(memory_space=pltpu.VMEM), any_space, any_space, any_space],
        out_specs=(any_space, any_space),
        scratch_shapes=[
            vm((count, steps, width), BF16),
            vm((PARTS, 256, steps), BF16),
            vm((PARTS, steps, 256), BF16),
            vm((count, 256, width), BF16),
            vm((count, 2, 64, 256), BF16),
            vm((count, 2, 64, width), BF16),
            vm((count, 2, 64, 256), BF16),
            vm((count, 64, width), BF16),
            vm((count, 3, 16, width), BF16),
            vm((PARTS, 64, width), BF16),
            vm((PARTS, RING, 16, width), BF16),
            vm((PARTS, 3, 16, width), BF16),
            vm((48, width), F32),
            vm((2, width, group), BF16),
            vm((2,) + mix_weight.shape, F32),
            vm((width, group), BF16),
            vm((2, 1024, 256), BF16),
            vm((2, 2, 48, 256), BF16),
            vm((PARTS, RING, 32, group), BF16),
            vm((PARTS, 2, 3, 256, group), BF16),
            dma((count,)), dma((3,)), dma((4,)), dma((3,)), dma((3,)),
            dma((count, 6)), dma((count, 6)), dma((count, 3)), dma((count, 3)),
            dma((PARTS, 3)), dma((PARTS, 3)),
            dma((PARTS, 3)), dma((PARTS, 3)), dma((PARTS, 3)), dma((PARTS, 3)),
            dma((PARTS, 2, 2 * RING)), dma((PARTS, 2, 2 * RING)),
        ],
        compiler_params=pltpu.CompilerParams(
            collective_id=0, has_side_effects=True, vmem_limit_bytes=60 * 1024 * 1024
        ),
        name="exchange",
    )(series, modes.reshape(1, -1), query_weight, mix_weight, out_weight)

    return pl.pallas_call(
        inverse_kernel,
        out_shape=jax.ShapeDtypeStruct((series_count, steps, group), BF16),
        in_specs=[any_space, any_space],
        out_specs=any_space,
        scratch_shapes=[
            vm((PARTS, steps, 256), BF16),
            vm((PARTS, 2, 3, 256, group), BF16),
            vm((series_count, steps, group), BF16),
            dma((PARTS,)), dma((PARTS,)), dma((series_count,)),
        ],
        compiler_params=pltpu.CompilerParams(vmem_limit_bytes=60 * 1024 * 1024),
        name="inverse",
    )(tables, gathered)


def solution(mesh):
    in_specs = (
        P(None, "tm", None),
        P(),
        P(None, "head"),
        P("tm", "head", None, None),
        P(None, "head"),
    )
    out_specs = P(None, "tm", "head")
    return jax.shard_map(body, mesh=mesh, in_specs=in_specs, out_specs=out_specs, check_vma=False)
```

```python
import functools
import math

import jax
import jax.numpy as jnp
from jax import lax
from jax.experimental import pallas as pl
from jax.experimental.pallas import tpu as pltpu
from jax.sharding import PartitionSpec as P

F32 = jnp.float32
BF16 = jnp.bfloat16
MESH = pl.DeviceIdType.MESH
RING = 4
PARTS = 3
PERIOD = 65536


def iota(shape, dim):
    return lax.broadcasted_iota(jnp.int32, shape, dim)


def one_hot(shape, wanted):
    return (iota(shape, 1) == wanted).astype(F32).astype(BF16)


def dot(a, b):
    return jnp.dot(a, b, preferred_element_type=F32)


def dot_nt(a, b):
    return lax.dot_general(a, b, (((1,), (1,)), ((), ())), preferred_element_type=F32)


def cos_sin(phase):
    phase = phase & (PERIOD - 1)
    quarter = (phase + PERIOD // 8) >> 14
    r = (phase - (quarter << 14)).astype(F32) * (2.0 * math.pi / PERIOD)
    q = r * r
    s = r * (1.0 + q * (-1 / 6 + q * (1 / 120 + q * (-1 / 5040 + q * (1 / 362880)))))
    c = 1.0 + q * (-0.5 + q * (1 / 24 + q * (-1 / 720 + q * (1 / 40320))))
    odd = (quarter & 1) == 1
    cos_value = jnp.where(odd, s, c)
    sin_value = jnp.where(odd, c, s)
    cos_value = jnp.where(((quarter + 1) & 2) != 0, -cos_value, cos_value)
    sin_value = jnp.where((quarter & 2) != 0, -sin_value, sin_value)
    return cos_value, sin_value


def stride_of(axis):
    return 16 - 12 * axis + 9 * ((axis * (axis - 1)) // 2)


def split(x):
    high = x.astype(BF16)
    low = (x - high.astype(F32)).astype(BF16)
    return high, low


def order_row(k, part):
    first, second, third, r = k // 64, (k // 16) % 4, (k // 4) % 4, k % 4
    if part == 0:
        return k
    if part == 1:
        return third * 64 + first * 16 + second * 4 + r
    return second * 64 + third * 16 + first * 4 + r


def exchange_kernel(
    scale, series, modes, wq_in, mix_in, wo_in, tab_out, gat_out,
    x, table, wide, sent, ra, rb, acc, s2, r2, v3, s3, r3, xs, wq, mix, wo, mw, mx, a1, gb,
    x_sem, w_sem, o_sem, p_send, p_recv, send1, recv1, send2, recv2, send3, recv3,
    g1_send, g1_recv, g2_send, g2_recv, g3_send, g3_recv,
):
    tm = lax.axis_index("tm")
    h = lax.axis_index("head")
    count = x.shape[0]

    def coord(axis):
        return lax.rem(lax.div(tm, stride_of(axis)), RING)

    def along(axis, distance):
        c = coord(axis)
        return tm + (lax.rem(c + distance, RING) - c) * stride_of(axis)

    def remote(src, dst, ssem, rsem, target):
        return pltpu.make_async_remote_copy(
            src_ref=src, dst_ref=dst, send_sem=ssem, recv_sem=rsem,
            device_id=(target, h), device_id_type=MESH,
        )

    def to_partner(src, dst, k):
        return pltpu.make_async_remote_copy(
            src_ref=src, dst_ref=dst, send_sem=p_send.at[k], recv_sem=p_recv.at[k],
            device_id=(tm, 1 - h), device_id_type=MESH,
        )

    def load_x(s):
        return pltpu.make_async_copy(series.at[h * count + s], x.at[s], x_sem.at[s])

    loads = [
        pltpu.make_async_copy(wq_in, wq.at[0], w_sem.at[0]),
        pltpu.make_async_copy(mix_in, mix.at[0], w_sem.at[1]),
        pltpu.make_async_copy(wo_in, wo, w_sem.at[2]),
    ]

    barrier = pltpu.get_barrier_semaphore()
    for axis in range(3):
        for d in range(1, RING):
            pl.semaphore_signal(barrier, inc=1, device_id=(along(axis, d), h), device_id_type=MESH)
    pl.semaphore_signal(barrier, inc=1, device_id=(tm, 1 - h), device_id_type=MESH)

    for s in range(count):
        load_x(s).start()
    for load in loads:
        load.start()

    rows = 256
    steps = x.shape[1]
    blocks = steps // 128
    first = tm * steps
    mode_high = jnp.broadcast_to((modes[...] >> 7).astype(F32), (128, 128)).astype(BF16)
    mode_low = jnp.broadcast_to((modes[...] & 127).astype(F32), (128, 128)).astype(BF16)
    pick = one_hot((rows, 128), iota((rows, 128), 0) // 2)
    by_row = (dot_nt(pick, mode_high) * 128.0 + dot_nt(pick, mode_low)).astype(jnp.int32)
    quarter_turn = (iota((rows, 128), 0) & 1) * (PERIOD // 4)
    cos_low, sin_low = cos_sin(by_row * iota((rows, 128), 1))
    cos_high, sin_high = cos_sin(
        by_row * (first + 128 * (iota((rows, 128), 1) & (blocks - 1))) + quarter_turn
    )
    for i in range(blocks):
        value = cos_high[:, i : i + 1] * cos_low - sin_high[:, i : i + 1] * sin_low
        table[0, :, pl.ds(128 * i, 128)] = value.astype(BF16)
    for part in range(1, PARTS):
        perm = one_hot((rows, rows), order_row(iota((rows, rows), 0), part))
        table[part] = dot(perm, table[0]).astype(BF16)

    pl.semaphore_wait(barrier, 10)
    to_partner(wq_in, wq.at[1], 0).start()
    to_partner(mix_in, mix.at[1], 1).start()

    def band(axis, d):
        c = lax.rem(coord(axis) + d, RING)
        return pl.ds(pl.multiple_of(c * 64, 64), 64)

    def stage1(s, way, kind):
        axis = lax.rem(s, PARTS)
        near = 1 if way == 0 else 3
        mine = pl.ds(256 * way, 256)
        other = pl.ds(256 * (1 - way), 256)
        slot = 2 * kind + way
        if kind == 0:
            src, dst = sent.at[s, band(axis, 2), mine], ra.at[s, way]
        elif kind == 1:
            src, dst = sent.at[s, band(axis, near), other], rb.at[s, way, :, other]
        else:
            src, dst = acc.at[s, way], rb.at[s, way, :, mine]
        return remote(src, dst, send1.at[s, slot], recv1.at[s, slot], along(axis, near))

    def forward(s, carry):
        load_x(s).wait()
        sent[s] = dot(table[lax.rem(s, PARTS)], x[s]).astype(BF16)
        for kind in range(2):
            for way in range(2):
                stage1(s, way, kind).start()
        return carry

    lax.fori_loop(0, count, forward, 0)

    def relay(s, carry):
        axis = lax.rem(s, PARTS)
        for way in range(2):
            stage1(s, way, 0).wait_recv()
            own = sent[s, band(axis, 1 if way == 0 else 3), pl.ds(256 * way, 256)]
            acc[s, way] = (own.astype(F32) + ra[s, way].astype(F32)).astype(BF16)
            stage1(s, way, 2).start()
        return carry

    lax.fori_loop(0, count, relay, 0)

    by_lane = (
        dot_nt(mode_high[0:8], pick) * 128.0 + dot_nt(mode_low[0:8], pick)
    ).astype(jnp.int32)
    turn_lane = (iota((8, rows), 1) & 1) * (PERIOD // 4)
    wide_cos, wide_sin = cos_sin(jnp.broadcast_to(by_lane[0:1], (128, rows)) * iota((128, rows), 0))
    top_cos, top_sin = cos_sin(by_lane * (first + 128 * (iota((8, rows), 0) & (blocks - 1))) + turn_lane)
    for i in range(blocks):
        value = top_cos[i : i + 1] * wide_cos - top_sin[i : i + 1] * wide_sin
        wide[0, pl.ds(128 * i, 128), :] = value.astype(BF16)
    for part in range(1, PARTS):
        perm = one_hot((rows, rows), order_row(iota((rows, rows), 0), part))
        wide[part] = dot_nt(wide[0], perm).astype(BF16)
    table_copy = pltpu.make_async_copy(wide, tab_out, o_sem.at[0])
    table_copy.start()

    for load in loads:
        load.wait()
    to_partner(wq_in, wq.at[1], 0).wait_recv()
    to_partner(mix_in, mix.at[1], 1).wait_recv()
    mw[...] = jnp.zeros_like(mw)
    left = iota((64, 128), 1) < 64
    for half in range(2):
        for m in range(2):
            for head in range(4):
                both = mix[half, m, head]
                turned = pltpu.roll(both, 64, 1)
                for kind in range(2):
                    value = both if kind == head % 2 else turned
                    keep = left if head % 2 == 0 else jnp.logical_not(left)
                    value = jnp.where(keep, value, 0.0).astype(BF16)
                    mw[half, pl.ds((2 * m + kind) * 256 + 64 * head, 64), pl.ds(128 * (head // 2), 128)] = value
    v3[...] = jnp.zeros_like(v3)

    def stage2(s, d):
        axis = lax.rem(s + 1, PARTS)
        c = lax.rem(coord(axis) + d, RING)
        return remote(
            s2.at[s, pl.ds(pl.multiple_of(c * 16, 16), 16), :], r2.at[s, d - 1],
            send2.at[s, d - 1], recv2.at[s, d - 1], along(axis, d),
        )

    def reduce1(s, carry):
        axis = lax.rem(s, PARTS)
        for kind in range(1, 3):
            for way in range(2):
                stage1(s, way, kind).wait_recv()
        total = sent[s, band(axis, 0), :].astype(F32) + rb[s, 0].astype(F32) + rb[s, 1].astype(F32)
        s2[s] = total.astype(BF16)
        for d in range(1, RING):
            stage2(s, d).start()
        return carry

    lax.fori_loop(0, count, reduce1, 0)

    def reduce2(s, carry):
        axis = lax.rem(s + 1, PARTS)
        for d in range(1, RING):
            stage2(s, d).wait_recv()
        own = s2[s, pl.ds(pl.multiple_of(coord(axis) * 16, 16), 16), :].astype(F32)
        total = own + r2[s, 0].astype(F32) + r2[s, 1].astype(F32) + r2[s, 2].astype(F32)
        row = pl.multiple_of(lax.div(s, PARTS) * 16, 16)
        v3[lax.rem(s, PARTS), pl.ds(row, 16), :] = total.astype(BF16)
        return carry

    lax.fori_loop(0, count, reduce2, 0)

    def stage3(part, d):
        axis = (part + 2) % PARTS
        c = lax.rem(coord(axis) + d, RING)
        return remote(
            s3.at[part, c], r3.at[part, d - 1],
            send3.at[part, d - 1], recv3.at[part, d - 1], along(axis, d),
        )

    k = iota((64, 64), 0)
    swap = one_hot((64, 64), ((k // 4) % 4) * 16 + (k // 16) * 4 + k % 4)
    for part in range(PARTS):
        turned = dot(swap, v3[part]).astype(BF16)
        for c in range(RING):
            s3[part, c] = turned[16 * c : 16 * c + 16]
        for d in range(1, RING):
            stage3(part, d).start()
    for part in range(PARTS):
        for d in range(1, RING):
            stage3(part, d).wait_recv()
        own = s3[part, coord((part + 2) % PARTS)].astype(F32)
        xs[pl.ds(16 * part, 16), :] = (
            own + r3[part, 0].astype(F32) + r3[part, 1].astype(F32) + r3[part, 2].astype(F32)
        )

    lhs = jnp.concatenate(split(xs[...]), axis=0)
    held = 16 * PARTS
    odd = (iota((held, 256), 0) & 1) == 1
    second = (iota((held, 256), 0) & 2) == 2
    for half in range(2):
        q = dot(lhs, wq[half])
        q = q[:held] + q[held:]
        crossed = jnp.where(odd, pltpu.roll(q, 1, 0), -pltpu.roll(q, held - 1, 0))
        pieces = [
            jnp.where(second, 0.0, q), jnp.where(second, 0.0, crossed),
            jnp.where(second, q, 0.0), jnp.where(second, crossed, 0.0),
        ]
        mixed = jnp.zeros((2 * held, 256), F32)
        for i in range(4):
            mixed = mixed + dot(jnp.concatenate(split(pieces[i]), axis=0), mw[half, pl.ds(256 * i, 256), :])
        mixed = (mixed[:held] + mixed[held:]).astype(BF16)
        mx[h, h if half == 0 else 1 - h] = mixed
    to_partner(mx.at[h], mx.at[h], 2).start()
    to_partner(mx.at[h], mx.at[h], 2).wait_recv()

    def gather1(part, d):
        axis = (part + 2) % PARTS
        c = coord(axis)
        return remote(
            a1.at[part, c], a1.at[part, c],
            g1_send.at[part, d - 1], g1_recv.at[part, d - 1], along(axis, d),
        )

    for group in range(2):
        g = dot(mx[group, 0], wo[pl.ds(0, 256), :]) + dot(mx[group, 1], wo[pl.ds(256, 256), :])
        g = (g * scale).astype(BF16)
        for part in range(PARTS):
            a1[part, coord((part + 2) % PARTS), pl.ds(16 * group, 16), :] = g[16 * part : 16 * part + 16]
    for part in range(PARTS):
        for d in range(1, RING):
            gather1(part, d).start()

    def gather2(part, d):
        at = gb.at[part, coord(part), :, coord((part + 1) % PARTS)]
        return remote(
            at, at,
            g2_send.at[part, d - 1], g2_recv.at[part, d - 1], along((part + 1) % PARTS, d),
        )

    k = iota((96, 128), 0)
    unswap = one_hot((96, 128), ((k // 4) % 4) * 32 + (k // 48) * 16 + ((k // 16) % 3) * 4 + k % 4)
    for part in range(PARTS):
        for d in range(1, RING):
            gather1(part, d).wait_recv()
        flat = jnp.concatenate([a1[part, c] for c in range(RING)], axis=0)
        turned = dot(unswap, flat).astype(BF16)
        for group in range(2):
            for j in range(PARTS):
                at = 48 * group + 16 * j
                gb[part, coord(part), group, coord((part + 1) % PARTS), j] = turned[at : at + 16]
        for d in range(1, RING):
            gather2(part, d).start()

    def gather3(part, way, group, relayed):
        near = 1 if way == 0 else 3
        c = lax.rem(coord(part) + (RING - near if relayed else 0), RING)
        at = gb.at[part, c, group]
        slot = 2 if relayed else group
        return remote(at, at, g3_send.at[part, way, slot], g3_recv.at[part, way, slot], along(part, near))

    for part in range(PARTS):
        for d in range(1, RING):
            gather2(part, d).wait_recv()
        for turn in range(2):
            for way in range(2):
                gather3(part, way, turn if way == 0 else 1 - turn, False).start()
    for part in range(PARTS):
        for way in range(2):
            gather3(part, way, way, False).wait_recv()
            gather3(part, way, way, True).start()
    gathered = []
    for part in range(PARTS):
        for way in range(2):
            gather3(part, way, 1 - way, False).wait_recv()
        for way in range(2):
            gather3(part, way, way, True).wait_recv()
        copy = pltpu.make_async_copy(gb.at[part], gat_out.at[part], o_sem.at[1 + part])
        copy.start()
        gathered.append(copy)

    def drain(s, carry):
        for kind in range(3):
            for way in range(2):
                stage1(s, way, kind).wait_send()
        for d in range(1, RING):
            stage2(s, d).wait_send()
        return carry

    lax.fori_loop(0, count, drain, 0)
    to_partner(wq_in, wq.at[1], 0).wait_send()
    to_partner(mix_in, mix.at[1], 1).wait_send()
    to_partner(mx.at[h], mx.at[h], 2).wait_send()
    for part in range(PARTS):
        for d in range(1, RING):
            stage3(part, d).wait_send()
            gather1(part, d).wait_send()
            gather2(part, d).wait_send()
        for way in range(2):
            gather3(part, way, 0, False).wait_send()
            gather3(part, way, 1, False).wait_send()
            gather3(part, way, way, True).wait_send()
    table_copy.wait()
    for copy in gathered:
        copy.wait()


def inverse_kernel(tab_in, gat_in, out, tab, gat, res, t_sem, g_sem, o_sem):
    def load_tab(part):
        return pltpu.make_async_copy(tab_in.at[part], tab.at[part], t_sem.at[part])

    def load_gat(part):
        return pltpu.make_async_copy(gat_in.at[part], gat.at[part], g_sem.at[part])

    def store(s):
        return pltpu.make_async_copy(res.at[s], out.at[s], o_sem.at[s])

    for part in range(PARTS):
        load_tab(part).start()
        load_gat(part).start()
    for part in range(PARTS):
        load_tab(part).wait()
        load_gat(part).wait()

        def step(j, carry):
            for group in range(2):
                s = 8 * group + 3 * j + part
                waves = gat[part, :, group, :, j].reshape(256, gat.shape[-1])
                res[s] = dot(tab[part], waves).astype(BF16)
                store(s).start()
            return carry

        lax.fori_loop(0, 3 - part // 2, step, 0)

    def drain(s, carry):
        store(s).wait()
        return carry

    lax.fori_loop(0, out.shape[0], drain, 0)


def body(series, modes, query_weight, mix_weight, out_weight):
    series_count, steps, width = series.shape
    group = query_weight.shape[1]
    count = series_count // 2
    scale = 1.0 / math.sqrt(PERIOD) / math.sqrt(modes.shape[0])
    hbm = pl.BlockSpec(memory_space=pltpu.HBM)
    any_space = pl.BlockSpec(memory_space=pl.ANY)
    dma = pltpu.SemaphoreType.DMA
    vm = pltpu.VMEM
    tables, gathered = pl.pallas_call(
        functools.partial(exchange_kernel, scale),
        out_shape=(
            jax.ShapeDtypeStruct((PARTS, steps, 256), BF16),
            jax.ShapeDtypeStruct((PARTS, RING, 2, RING, 3, 16, group), BF16),
        ),
        in_specs=[hbm, pl.BlockSpec(memory_space=pltpu.VMEM), hbm, hbm, hbm],
        out_specs=(any_space, any_space),
        scratch_shapes=[
            vm((count, steps, width), BF16),
            vm((PARTS, 256, steps), BF16),
            vm((PARTS, steps, 256), BF16),
            vm((count, 256, width), BF16),
            vm((count, 2, 64, 256), BF16),
            vm((count, 2, 64, width), BF16),
            vm((count, 2, 64, 256), BF16),
            vm((count, 64, width), BF16),
            vm((count, 3, 16, width), BF16),
            vm((PARTS, 64, width), BF16),
            vm((PARTS, RING, 16, width), BF16),
            vm((PARTS, 3, 16, width), BF16),
            vm((48, width), F32),
            vm((2, width, group), BF16),
            vm((2,) + mix_weight.shape, F32),
            vm((width, group), BF16),
            vm((2, 1024, 256), BF16),
            vm((2, 2, 48, 256), BF16),
            vm((PARTS, RING, 32, group), BF16),
            vm((PARTS, RING, 2, RING, 3, 16, group), BF16),
            dma((count,)), dma((3,)), dma((4,)), dma((3,)), dma((3,)),
            dma((count, 6)), dma((count, 6)), dma((count, 3)), dma((count, 3)),
            dma((PARTS, 3)), dma((PARTS, 3)),
            dma((PARTS, 3)), dma((PARTS, 3)), dma((PARTS, 3)), dma((PARTS, 3)),
            dma((PARTS, 2, 3)), dma((PARTS, 2, 3)),
        ],
        compiler_params=pltpu.CompilerParams(
            collective_id=0, has_side_effects=True, vmem_limit_bytes=50 * 1024 * 1024
        ),
        name="exchange",
    )(series, modes.reshape(1, -1), query_weight, mix_weight, out_weight)

    return pl.pallas_call(
        inverse_kernel,
        out_shape=jax.ShapeDtypeStruct((series_count, steps, group), BF16),
        in_specs=[any_space, any_space],
        out_specs=hbm,
        scratch_shapes=[
            vm((PARTS, steps, 256), BF16),
            vm((PARTS, RING, 2, RING, 3, 16, group), BF16),
            vm((series_count, steps, group), BF16),
            dma((PARTS,)), dma((PARTS,)), dma((series_count,)),
        ],
        compiler_params=pltpu.CompilerParams(vmem_limit_bytes=40 * 1024 * 1024),
        name="inverse",
    )(tables, gathered)


def solution(mesh):
    in_specs = (
        P(None, "tm", None),
        P(),
        P(None, "head"),
        P("tm", "head", None, None),
        P(None, "head"),
    )
    out_specs = P(None, "tm", "head")
    return jax.shard_map(body, mesh=mesh, in_specs=in_specs, out_specs=out_specs, check_vma=False)
```
